32 devices in a mesh: freq: 4 (over y, x), rec: 8 (over z, core).
Axes of the slice: x: 2, y: 2, z: 4, core: 2. Of those that a mesh axis runs over, the one named last changes fastest.
Arguments:
- response: bfloat16 [128, 2, 1792, 1792], P('freq', None, 'rec'), may hold values from -1 to 1, as said below
- direct: float32 [1792, 32, 256], P('rec', 'freq'), may hold values from -6 to 6
- onset: int32 [1792, 32], P('rec', 'freq'), may hold values from 16 to 128
Outputs:
- upgoing: float32 [1792, 32, 256], P('rec', 'freq')
- coda: float32 [1792, 32, 256], P('rec', 'freq')
The draws below stay inside these ranges and needn't reach their ends.
Inputs may be any that keep to these rules, and one draw needn't show every extreme that they name: response[k, c, r, s] = response[k, c, s, r] for every frequency and part (source-receiver reciprocity).
All inputs are finite; a program needn't handle non-finite values.
Results may differ from the reference program's by a relative error of at most 0.023.
Values may be sent and summed in bfloat16 or wider, within the bound.
No kernel may reach another device: no remote copies, remote signals or barrier semaphores. Data moves between devices by JAX's collectives and lax.ppermute only.
A program may use at most 128 MiB of HBM per device.

```python
import math
import jax
import jax.numpy as jnp
from jax import lax

NS = 1792
NF = 128
NT = 256
NV = 32
ITERS = 2


def draw_response(key, part):
    subkeys = jax.random.split(jax.random.fold_in(key, 17), NF)

    def per_frequency(subkey):
        entries = jnp.clip(jax.random.normal(subkey, (2, NS, NS), jnp.float32), -4.0, 4.0)
        paired = (entries + jnp.swapaxes(entries, 1, 2)) * 0.5 ** 0.5
        return (paired * (2.0 * NS) ** (-0.5)).astype(jnp.bfloat16)
    return lax.map(per_frequency, subkeys)


def plant(result, own_key, smallest, top_value):
    extent = result.shape
    spot = [jax.random.randint(jax.random.fold_in(own_key, axis), (), 0, extent[axis]) for axis in range(len(extent))]
    result = result.at[tuple(spot)].set(smallest)
    longest = extent.index(max(extent))
    spot[longest] = (spot[longest] + 1) % extent[longest]
    return result.at[tuple(spot)].set(top_value)


def level_of(own_key, extent, pieces, smallest, high):
    factor_of, own = 1.0, jax.random.fold_in(own_key, 6)
    for position, blocks in pieces:
        draws = jnp.exp(jax.random.uniform(jax.random.fold_in(own, position), (blocks,), jnp.float32, smallest / len(pieces), high / len(pieces)))
        factor_of = factor_of * jnp.repeat(draws, extent[position] // blocks).reshape([-1 if axis == position else 1 for axis in range(len(extent))])
    return factor_of


def normal_values(rng, extent, scale, most, cuts=(), held_as=jnp.bfloat16):
    drawn = scale * jax.random.normal(rng, extent, jnp.float32)
    if cuts:
        drawn = drawn * level_of(rng, extent, cuts, -0.22, 0.18)
    return jnp.clip(drawn, -most, most).astype(held_as)


def setup_inputs(seed: int = 0) -> dict:
    key_list = jax.random.split(jax.random.key(seed), 4)
    response = draw_response(jax.random.fold_in(key_list[3], 71), 0)
    direct = normal_values(key_list[1], (NS, NV, NT), 1.0, 6.0, ((0, 8), (1, 4)), jnp.float32)
    onset = plant(jax.random.randint(key_list[2], (NS, NV), NT // 16, NT // 2 + 1), jax.random.fold_in(key_list[2], 1), NT // 16, (NT // 2 + 1) - 1).astype(jnp.int32)
    return {"response": response, "direct": direct, "onset": onset}


def spectral_tables(length, count):
    samples = jnp.arange(length, dtype=jnp.int32)
    frequency_bins = jnp.arange(1, count + 1, dtype=jnp.int32)
    phase = ((samples[:, None] * frequency_bins[None, :]) % length).astype(jnp.float32) * (2.0 * math.pi / length)
    cosine = jnp.cos(phase)
    sine = jnp.sin(phase)
    forward = jnp.concatenate([cosine, -sine], axis=1)
    inverse = jnp.concatenate([cosine.T, -sine.T], axis=0) * (2.0 / length)
    return forward, inverse


def make_window(onset, length):
    samples = jnp.arange(length, dtype=jnp.int32)
    folded = jnp.minimum(samples, length - samples)
    return (folded[None, None, :] < onset[:, :, None]).astype(jnp.float32)


def to_spectrum(field, forward):
    packed = jnp.dot(field, forward, precision=lax.Precision.HIGHEST).astype(jnp.bfloat16)
    return packed.reshape(field.shape[0], field.shape[1], 2, forward.shape[1] // 2)


def to_time(spectra, inverse):
    flat = spectra.reshape(spectra.shape[0], spectra.shape[1], -1).astype(jnp.float32)
    return jnp.dot(flat, inverse, precision=lax.Precision.HIGHEST)


def convolve(response, spectra, adjoint):
    moved = jnp.transpose(spectra, (3, 0, 1, 2))

    def per_frequency(unused_state, frequency_slice):
        matrix, vectors = frequency_slice
        real_matrix = matrix[0]
        imag_matrix = matrix[1]
        if adjoint:
            real_matrix = real_matrix.T
            imag_matrix = -imag_matrix.T
        vec_real = vectors[:, :, 0]
        vec_imag = vectors[:, :, 1]
        out_real = jnp.dot(real_matrix, vec_real, preferred_element_type=jnp.float32) - jnp.dot(imag_matrix, vec_imag, preferred_element_type=jnp.float32)
        out_imag = jnp.dot(real_matrix, vec_imag, preferred_element_type=jnp.float32) + jnp.dot(imag_matrix, vec_real, preferred_element_type=jnp.float32)
        return unused_state, jnp.stack([out_real, out_imag], axis=2)

    unused_final, stacked = lax.scan(per_frequency, jnp.zeros((), jnp.float32), (response, moved))
    return jnp.transpose(stacked, (1, 2, 3, 0)).astype(jnp.bfloat16)


def reference(response, direct, onset):
    forward, inverse = spectral_tables(NT, NF)
    window = make_window(onset, NT)
    coda = jnp.zeros_like(direct)
    upgoing = coda
    for iteration in range(ITERS):
        downgoing = direct + coda
        spectra = to_spectrum(downgoing, forward)
        reflected = convolve(response, spectra, False)
        upgoing = window * to_time(reflected, inverse)
        spectra_up = to_spectrum(upgoing, forward)
        returned = convolve(response, spectra_up, True)
        coda = window * to_time(returned, inverse)
    return upgoing, coda
```

```python
import functools
import math

import jax
import jax.numpy as jnp
from jax import lax
from jax.experimental import pallas as pl
from jax.experimental.pallas import tpu as pltpu
from jax.sharding import PartitionSpec as P

ITERS = 2
LANES = 128
VMEM_LIMIT = 60 * 1024 * 1024


def spectral_tables(length, count):
    samples = jnp.arange(length, dtype=jnp.int32)
    bins = jnp.arange(1, count + 1, dtype=jnp.int32)
    phase = (bins[:, None] * samples[None, :] % length).astype(jnp.float32) * (
        2.0 * math.pi / length
    )
    table = jnp.stack([jnp.cos(phase), -jnp.sin(phase)], axis=1).reshape(2 * count, length)
    return table, table * (2.0 / length)


def convolve_kernel(conj_sign, virtual, r_ref, x_ref, o_ref, acc_ref):
    owners, _, lanes = x_ref.shape
    rows = r_ref.shape[1] // 2
    count = lanes // (2 * virtual)
    step = pl.program_id(0) % count
    lane = lax.broadcasted_iota(jnp.int32, (2 * rows, 2 * lanes), 1)
    mine = (lane % lanes) // (2 * virtual) == step
    for first in range(0, owners, 2):
        weights = jnp.concatenate([x_ref[first], x_ref[first + 1]], axis=1)
        product = jnp.dot(r_ref[0], weights, preferred_element_type=jnp.float32)
        at = (slice(None), slice(first * lanes, (first + 2) * lanes))
        acc_ref[at] = jnp.where(mine, product, acc_ref[at])

    @pl.when(step == count - 1)
    def _():
        lane = lax.broadcasted_iota(jnp.int32, (rows, lanes), 1)
        is_real = (lane // virtual) % 2 == 0
        for owner in range(owners):
            columns = slice(owner * lanes, (owner + 1) * lanes)
            by_real = acc_ref[:rows, columns]
            by_imag = acc_ref[rows:, columns]
            above = pltpu.roll(by_imag, lanes - virtual, 1)
            below = pltpu.roll(by_imag, virtual, 1)
            crossed = jnp.where(is_real, -conj_sign * above, conj_sign * below)
            o_ref[owner] = (by_real + crossed).astype(o_ref.dtype)


def convolve(response, spectra, first, virtual, conj_sign):
    owners, sources, width = spectra.shape
    rows = response.shape[1] // 2
    group = LANES // (2 * virtual)
    count = width // (2 * virtual)
    return pl.pallas_call(
        functools.partial(convolve_kernel, conj_sign, virtual),
        out_shape=jax.ShapeDtypeStruct((owners, rows, width), jnp.bfloat16),
        grid=(count,),
        in_specs=[
            pl.BlockSpec((1, 2 * rows, sources), lambda k: (first * group + k, 0, 0)),
            pl.BlockSpec((owners, sources, LANES), lambda k: (0, 0, k // group)),
        ],
        out_specs=pl.BlockSpec((owners, rows, LANES), lambda k: (0, 0, k // group)),
        scratch_shapes=[pltpu.VMEM((2 * rows, owners * LANES), jnp.float32)],
        compiler_params=pltpu.CompilerParams(
            dimension_semantics=("arbitrary",), vmem_limit_bytes=VMEM_LIMIT
        ),
        cost_estimate=pl.CostEstimate(
            flops=count * 4 * rows * sources * owners * LANES,
            bytes_accessed=count * 4 * rows * sources,
            transcendentals=0,
        ),
    )(response, spectra)


def transform_kernel(sizes, has_spectra, has_direct, has_field, has_next, *refs):
    refs = list(refs)
    take = lambda n: [refs.pop(0) for _ in range(n)]
    received = take(len(sizes)) if has_spectra else []
    onset_ref, = take(1) if has_spectra else [None]
    direct_ref, = take(1) if has_direct else [None]
    inverse_ref, = take(1) if has_spectra else [None]
    forward_ref, = take(1) if has_next else [None]
    field_ref, = take(1) if has_field else [None]
    sending = take(len(sizes)) if has_next else []
    scratch, = take(1)
    bins, length = (inverse_ref if has_spectra else forward_ref).shape
    virtual = scratch.shape[1] // bins
    rows = (received or sending)[0].shape[1]
    tiles = [(n, n * LANES, min(LANES, rows - n * LANES)) for n in range(scratch.shape[0])]
    spare = len(tiles) * LANES - rows
    groups = [(n, i * LANES) for n, size in enumerate(sizes) for i in range(size)]
    if has_spectra:
        for owner in range(received[0].shape[0]):
            for place, (chunk, lane) in enumerate(groups):
                at = (owner * len(groups) + place) * LANES
                for n, start, width in tiles:
                    block = received[chunk][owner, start : start + width, lane : lane + LANES]
                    scratch[n, at : at + LANES, :width] = block.astype(jnp.float32).T
        sample = lax.broadcasted_iota(jnp.int32, (rows, length), 1)
        folded = jnp.minimum(sample, length - sample)
    for v in range(virtual):
        mine = pl.ds(v, bins, stride=virtual)
        field = None
        if has_spectra:
            spectra = jnp.concatenate([scratch[n, mine, :] for n, _, _ in tiles], axis=1)
            field = lax.dot_general(
                spectra[:, :rows],
                inverse_ref[...],
                (((0,), (0,)), ((), ())),
                precision=lax.Precision.HIGHEST,
                preferred_element_type=jnp.float32,
            )
            field = jnp.where(folded < onset_ref[:, v : v + 1], field, 0.0)
            if has_field:
                field_ref[:, v, :] = field
        if has_direct:
            direct = direct_ref[:, v, :]
            field = direct if field is None else direct + field
        if has_next:
            if spare:
                field = jnp.concatenate([field, jnp.zeros((spare, length), jnp.float32)], axis=0)
            spectra = lax.dot_general(
                forward_ref[...],
                field,
                (((1,), (1,)), ((), ())),
                precision=lax.Precision.HIGHEST,
                preferred_element_type=jnp.float32,
            )
            for n, start, _ in tiles:
                scratch[n, mine, :] = spectra[:, start : start + LANES]
    if has_next:
        for owner in range(sending[0].shape[0]):
            for place, (chunk, lane) in enumerate(groups):
                at = (owner * len(groups) + place) * LANES
                for n, start, width in tiles:
                    block = scratch[n, at : at + LANES, :].T[:width].astype(jnp.bfloat16)
                    sending[chunk][owner, start : start + width, lane : lane + LANES] = block


def transform(received, onset, direct, forward, inverse, shape, sizes, owners, has_field, has_next):
    rows, virtual, length = shape
    bins = forward.shape[0]
    has_spectra = received is not None
    operands = []
    if has_spectra:
        operands += [*received, onset]
    if direct is not None:
        operands.append(direct)
    if has_spectra:
        operands.append(inverse)
    if has_next:
        operands.append(forward)
    outs = []
    if has_field:
        outs.append(jax.ShapeDtypeStruct(shape, jnp.float32))
    if has_next:
        outs += [jax.ShapeDtypeStruct((owners, rows, n * LANES), jnp.bfloat16) for n in sizes]
    results = pl.pallas_call(
        functools.partial(
            transform_kernel, sizes, has_spectra, direct is not None, has_field, has_next
        ),
        out_shape=outs,
        scratch_shapes=[pltpu.VMEM((pl.cdiv(rows, LANES), bins * virtual, LANES), jnp.float32)],
        compiler_params=pltpu.CompilerParams(vmem_limit_bytes=VMEM_LIMIT),
    )(*operands)
    results = list(results)
    field = results.pop(0) if has_field else None
    return field, results


def exchange(block):
    return lax.all_to_all(block, "freq", split_axis=0, concat_axis=0, tiled=True)


def body(response, direct, onset):
    owners = lax.axis_size("freq")
    rows, virtual, length = direct.shape
    band = response.shape[0]
    groups = band * 2 * virtual // LANES
    sizes = (groups - 1, 1) if groups > 1 else (1,)
    response = response.reshape(band, 2 * rows, response.shape[3])
    forward, inverse = spectral_tables(length, band * owners)
    shared = (forward, inverse, direct.shape, sizes, owners)
    _, sending = transform(None, None, direct, *shared, False, True)
    fields = []
    for half in range(2 * ITERS):
        adjoint = half % 2
        last = half == 2 * ITERS - 1
        gathered = [
            lax.all_gather(exchange(block), "rec", axis=1, tiled=True) for block in sending
        ]
        products = [
            convolve(response, block, sum(sizes[:n]), virtual, -1.0 if adjoint else 1.0)
            for n, block in enumerate(gathered)
        ]
        received = [exchange(block) for block in products]
        field, sending = transform(
            received,
            onset,
            direct if adjoint and not last else None,
            *shared,
            half >= 2 * ITERS - 2,
            not last,
        )
        fields.append(field)
    return fields[-2], fields[-1]


def solution(mesh):
    placed = (P("freq", None, "rec", None), P("rec", "freq", None), P("rec", "freq"))
    return jax.shard_map(
        body,
        mesh=mesh,
        in_specs=placed,
        out_specs=(P("rec", "freq", None), P("rec", "freq", None)),
        check_vma=False,
    )
```
